512 devices in a mesh: row: 32 (over z, x), col: 16 (over y, core).
Axes of the slice: x: 4, y: 8, z: 8, core: 2. Of those that a mesh axis runs over, the one named last changes fastest.
Arguments:
- features: float32 [24576, 64], P('row'), may hold values from -6 to 6
- noise: float32 [24576], P('row'), may hold values from 0.1 to 1
- tile_map: int32 [192], replicated, may hold values from 0 to 191, each once
- panel_tile: int32 [1], replicated, may hold values from 0 to 143
Outputs:
- panel: float32 [24576, 128], P('row')
- trailing: float32 [24576, 24576], P('row', 'col')
The draws below stay inside these ranges and needn't reach their ends.
Inputs may be any that keep to these rules, and one draw needn't show every extreme that they name: `tile_map`: a permutation: every global tile 0 to 191 is held by exactly one slot.
All inputs are finite; a program needn't handle non-finite values.
Results may differ from the reference program's by a relative error of at most 0.0003.
Values sent between devices are 32-bit elements; how exact they have to be, the bound alone decides.
No kernel may reach another device: no remote copies, remote signals or barrier semaphores. Data moves between devices by JAX's collectives and lax.ppermute only.
A program may use at most 64 MiB of HBM per device.

```python
import math
import jax
import jax.numpy as jnp
from jax import lax

TILE = 128
FEAT = 64
NT = 192
M = 24576


def block_scale(stream_key, dims, cuts, smallest, largest):
    level, own = 1.0, jax.random.fold_in(stream_key, 6)
    for position, parts in cuts:
        steps = jnp.exp(jax.random.uniform(jax.random.fold_in(own, position), (parts,), jnp.float32, smallest / len(cuts), largest / len(cuts)))
        level = level * jnp.repeat(steps, dims[position] // parts).reshape([-1 if axis == position else 1 for axis in range(len(dims))])
    return level


def gaussian(own_key, extent, width, most, cuts=(), held_as=jnp.bfloat16):
    result = jax.random.normal(own_key, extent, jnp.float32) * width
    if len(cuts) > 0:
        result = block_scale(own_key, extent, cuts, -0.22, 0.18) * result
    return jnp.clip(result, min=-most, max=most).astype(held_as)


def setup_inputs(seed: int = 0) -> dict:
    keys = jax.random.split(jax.random.key(seed), 5)
    features = gaussian(keys[0], (M, FEAT), 1.0, 6.0, ((0, 32),), jnp.float32)
    noise = jnp.clip(jnp.exp(math.log(1.0) - 2.3025851 * jax.random.uniform(keys[1], (M,), jnp.float32) ** block_scale(keys[1], (M,), ((0, 32),), -0.2, 0.2)), 0.1, 1.0)
    tile_map = jax.random.permutation(keys[2], NT).astype(jnp.int32)
    panel_tile = jax.random.randint(keys[3], (1,), 0, 3 * NT // 4).astype(jnp.int32)
    return dict(features=features, noise=noise, tile_map=tile_map, panel_tile=panel_tile)


HIGHEST_MODE = lax.Precision.HIGHEST

def kernel_block(left_rows, right_rows):
    inner_part = jnp.dot(left_rows.astype(jnp.float32), right_rows.T.astype(jnp.float32), precision=HIGHEST_MODE, preferred_element_type=jnp.float32)
    left_sq = jnp.sum(left_rows * left_rows, axis=1)
    right_sq = jnp.sum(right_rows * right_rows, axis=1)
    return jnp.exp((2.0 * inner_part - left_sq[:, None] - right_sq[None, :]) / left_rows.shape[1])

def pivot_inverse(pivot_feat, pivot_noise):
    kernel_part = kernel_block(pivot_feat, pivot_feat) + jnp.diag(pivot_noise)
    lower_factor = jnp.linalg.cholesky(kernel_part)
    identity = jnp.eye(kernel_part.shape[0], dtype=kernel_part.dtype)
    return jax.scipy.linalg.solve_triangular(lower_factor, identity, lower=True)

def panel_piece(feat_rows, noise_rows, tile_of_row, offset_of_row, pivot_feat, inverse, pivot_tile):
    tile_width = pivot_feat.shape[0]
    kernel_part = kernel_block(feat_rows, pivot_feat)
    on_diagonal = (tile_of_row == pivot_tile)[:, None] & (offset_of_row[:, None] == jnp.arange(tile_width, dtype=jnp.int32)[None, :])
    kernel_part = kernel_part + jnp.where(on_diagonal, noise_rows[:, None], 0.0)
    factor = jnp.dot(kernel_part.astype(jnp.float32), inverse.T.astype(jnp.float32), precision=HIGHEST_MODE, preferred_element_type=jnp.float32)
    return jnp.where((tile_of_row >= pivot_tile)[:, None], factor, 0.0)

def trailing_block(row_feat, row_noise, row_panel, row_tile, row_offset, col_feat, col_panel, col_tile, col_offset, pivot_tile):
    kernel_part = kernel_block(row_feat, col_feat)
    same_entry = (row_tile[:, None] == col_tile[None, :]) & (row_offset[:, None] == col_offset[None, :])
    kernel_part = kernel_part + jnp.where(same_entry, row_noise[:, None], 0.0)
    kernel_part = kernel_part - jnp.dot(row_panel.astype(jnp.float32), col_panel.T.astype(jnp.float32), precision=HIGHEST_MODE, preferred_element_type=jnp.float32)
    live_entry = (row_tile[:, None] >= col_tile[None, :]) & (col_tile[None, :] > pivot_tile)
    return jnp.where(live_entry, kernel_part, 0.0)

def reference(features, noise, tile_map, panel_tile):
    tile_width = TILE
    pivot_tile = panel_tile[0]
    tile_count = tile_map.shape[0]
    slot_ids = jnp.arange(tile_count, dtype=jnp.int32)
    pivot_slot = jnp.sum(jnp.where(tile_map == pivot_tile, slot_ids, 0)).astype(jnp.int32)
    pivot_feat = lax.dynamic_slice_in_dim(features, pivot_slot * tile_width, tile_width, 0)
    pivot_noise = lax.dynamic_slice_in_dim(noise, pivot_slot * tile_width, tile_width, 0)
    inverse = pivot_inverse(pivot_feat, pivot_noise)
    tile_of_row = jnp.repeat(tile_map, tile_width)
    offset_of_row = jnp.tile(jnp.arange(tile_width, dtype=jnp.int32), tile_count)
    panel_rows = panel_piece(features, noise, tile_of_row, offset_of_row, pivot_feat, inverse, pivot_tile)

    def one_tile(slot_index):
        first_row = (slot_index * tile_width).astype(jnp.int32)
        row_feat = lax.dynamic_slice_in_dim(features, first_row, tile_width, 0)
        row_noise = lax.dynamic_slice_in_dim(noise, first_row, tile_width, 0)
        row_panel = lax.dynamic_slice_in_dim(panel_rows, first_row, tile_width, 0)
        row_tile = lax.dynamic_slice_in_dim(tile_of_row, first_row, tile_width, 0)
        row_offset = lax.dynamic_slice_in_dim(offset_of_row, first_row, tile_width, 0)
        return trailing_block(row_feat, row_noise, row_panel, row_tile, row_offset, features, panel_rows, tile_of_row, offset_of_row, pivot_tile)
    stacked = lax.map(one_tile, slot_ids)
    trailing = stacked.reshape(tile_count * tile_width, tile_count * tile_width)
    return (panel_rows, trailing)
```

```python
import jax
import jax.numpy as jnp
from jax import lax
from jax.experimental import pallas as pl
from jax.experimental.pallas import tpu as pltpu
from jax.sharding import PartitionSpec as P

TILE = 128
FEAT = 64
HIGHEST_MODE = lax.Precision.HIGHEST
F32 = jnp.float32
BF16 = jnp.bfloat16
VMEM = pltpu.VMEM
SMEM = pltpu.SMEM
CHUNK = 256


def vspec():
    return pl.BlockSpec(memory_space=VMEM)


def sspec():
    return pl.BlockSpec(memory_space=SMEM)


def pivot_slot_of(map_ref, panel_ref, tile_count):
    pivot = panel_ref[0]

    def step(s, slot):
        return jnp.where(map_ref[s] == pivot, s, slot)

    return lax.fori_loop(0, tile_count, step, jnp.int32(0), unroll=16)


def pack_kernel(tiles_here, map_ref, panel_ref, feat_ref, noise_ref, out_ref, slot_ref):
    slot = pivot_slot_of(map_ref, panel_ref, map_ref.shape[0])
    slot_ref[0] = slot
    local = jnp.clip(slot - lax.axis_index("row") * tiles_here, 0, tiles_here - 1)
    rows = feat_ref.shape[1]
    extra = jnp.broadcast_to(noise_ref[pl.ds(local, 1), :], (2, TILE))
    for r in range(out_ref.shape[0]):
        out_ref[r, :, :rows] = feat_ref[2 * r : 2 * r + 2, :]
        out_ref[r, :, rows:] = extra


def pick_kernel(tiles_here, blocks_per_col, slot_ref, got_ref, out_ref, noise_ref):
    slot = slot_ref[0]
    rows = tiles_here * TILE
    first = lax.axis_index("col") * blocks_per_col
    owner = slot // tiles_here
    offset = pl.multiple_of((slot - owner * tiles_here) * TILE, TILE)
    noise_ref[...] = got_ref[owner, 0:1, rows:]
    parts = [got_ref[first + m, :, :rows] for m in range(blocks_per_col)]
    parts.append(got_ref[owner, :, pl.ds(offset, TILE)])
    for r in range(out_ref.shape[0]):
        at = 0
        for part in parts:
            out_ref[r, :, at : at + part.shape[1]] = part
            at += part.shape[1]


def split2(x):
    hi = x.astype(BF16).astype(F32)
    return hi, x - hi


def split3(x):
    a = x.astype(BF16).astype(F32)
    b = (x - a).astype(BF16).astype(F32)
    return a, b, x - a - b


def tail(norm, mine_first):
    n = norm.shape[1]
    at = lax.broadcasted_iota(jnp.int32, (16, n), 0)
    a, b, c = (jnp.broadcast_to(-v, (16, n)) for v in split3(norm))
    base = 0 if mine_first else 3
    out = jnp.where((at >= 3 - base) & (at < 6 - base), 1.0, 0.0)
    for i, v in enumerate((a, b, c)):
        out = jnp.where(at == base + i, v, out)
    return out


def left_side(feat_t):
    norm = jnp.sum(feat_t * feat_t, axis=0, keepdims=True) * (1.0 / FEAT)
    hi, lo = split2(feat_t)
    return jnp.concatenate([hi, hi, lo, tail(norm, True)], axis=0)


def right_side(feat_t):
    norm = jnp.sum(feat_t * feat_t, axis=0, keepdims=True) * (1.0 / FEAT)
    hi, lo = split2(feat_t * (2.0 / FEAT))
    return jnp.concatenate([hi, lo, hi, tail(norm, False)], axis=0).astype(BF16)


def inverse_factor(gram, inv_ref):
    w = [gram[8 * t : 8 * t + 8, :] for t in range(TILE // 8)]
    lane = lax.broadcasted_iota(jnp.int32, (1, TILE), 1)
    sub = lax.broadcasted_iota(jnp.int32, (8, 1), 0)
    for j in range(TILE):
        jt, js = divmod(j, 8)
        row = w[jt][js : js + 1, :]
        piv = row[:, j : j + 1]
        scaled = jnp.where(lane == j, piv + 1.0, row) * (1.0 / piv)
        inv_ref[j : j + 1, :] = jnp.where(
            lane < j, row, jnp.where(lane == j, 1.0, 0.0)
        ) * lax.rsqrt(piv)
        for t in range(jt, TILE // 8):
            col = w[t][:, j : j + 1]
            if t == jt:
                if js == 7:
                    continue
                col = jnp.where(sub > js, col, 0.0)
            w[t] = w[t] - col * scaled


def dot(a, b, precision=None):
    return jnp.dot(a, b, precision=precision, preferred_element_type=F32)


def step_kernel(
    tiles_here,
    map_ref,
    panel_tile_ref,
    slot_ref,
    got_ref,
    pivot_noise_ref,
    feat_ref,
    noise_ref,
    panel_ref,
    out_ref,
    all_t,
    inv_ref,
    left_ref,
    right_ref,
    row_panel_ref,
    col_panel_ref,
):
    chunk = pl.program_id(0)
    rows = tiles_here * TILE
    cols = right_ref.shape[1]
    tiles_across = cols // TILE
    slot = slot_ref[0]
    pivot = panel_tile_ref[0]
    first_row_slot = lax.axis_index("row") * tiles_here
    first_col_slot = lax.axis_index("col") * tiles_across
    at_row = lax.broadcasted_iota(jnp.int32, (TILE, TILE), 0)
    at_col = lax.broadcasted_iota(jnp.int32, (TILE, TILE), 1)
    diagonal = at_row == at_col

    @pl.when(chunk == 0)
    def _():
        for r in range(got_ref.shape[0]):
            all_t[2 * r : 2 * r + 2, :] = got_ref[r]
        pivot_t = all_t[:, cols:]
        pivot_norm = jnp.sum(pivot_t * pivot_t, axis=0, keepdims=True)
        pivot_rows = pivot_t.T
        pivot_norm_col = jnp.sum(pivot_rows * pivot_rows, axis=1, keepdims=True)
        inner = dot(pivot_rows, pivot_t, HIGHEST_MODE)
        gram = jnp.exp((2.0 * inner - pivot_norm_col - pivot_norm) * (1.0 / FEAT))
        pivot_noise = jnp.where(diagonal, pivot_noise_ref[...], 0.0)
        inverse_factor(gram + pivot_noise, inv_ref)
        inverse = inv_ref[...]
        inverse_t = inverse.T
        pivot_left = left_side(pivot_t).T.astype(BF16)
        pivot_right = right_side(pivot_t)
        right = right_side(all_t[:, :cols])
        right_ref[...] = right
        for j in range(tiles_across):
            here = slice(j * TILE, (j + 1) * TILE)
            kern = jnp.exp(dot(pivot_left, right[:, here]))
            kern = kern + jnp.where(first_col_slot + j == slot, pivot_noise, 0.0)
            hi, lo = split2(dot(inverse, kern, HIGHEST_MODE))
            col_panel_ref[:, here] = jnp.concatenate([hi, lo, hi], axis=0).astype(BF16)
        for i in range(tiles_here):
            here = slice(i * TILE, (i + 1) * TILE)
            left = left_side(feat_ref[:, here]).T.astype(BF16)
            left_ref[here, :] = left
            kern = jnp.exp(dot(left, pivot_right))
            kern = kern + jnp.where(first_row_slot + i == slot, pivot_noise, 0.0)
            factor = dot(kern, inverse_t, HIGHEST_MODE)
            factor = jnp.where(map_ref[first_row_slot + i] >= pivot, factor, 0.0)
            panel_ref[here, :] = factor
            hi, lo = split2(factor)
            row_panel_ref[here, :] = jnp.concatenate([hi, hi, lo], axis=1).astype(BF16)

    across = pl.ds(pl.multiple_of(chunk * CHUNK, CHUNK), CHUNK)
    right = right_ref[:, across]
    col_panel = col_panel_ref[:, across]
    per_chunk = CHUNK // TILE
    for i in range(tiles_here):
        here = slice(i * TILE, (i + 1) * TILE)
        value = jnp.exp(dot(left_ref[here, :], right)) - dot(row_panel_ref[here, :], col_panel)
        row_tile = map_ref[first_row_slot + i]
        for h in range(per_chunk):
            col_slot = first_col_slot + chunk * per_chunk + h
            col_tile = map_ref[col_slot]
            live = (row_tile >= col_tile) & (col_tile > pivot)
            part = slice(h * TILE, (h + 1) * TILE)
            out_ref[here, part] = jnp.where(live, value[:, part], 0.0)

            @pl.when((first_row_slot + i == col_slot) & live)
            def _():
                out_ref[here, part] += jnp.where(diagonal, noise_ref[i : i + 1, :], 0.0)


def shards(features, noise, tile_map, panel_tile):
    rows_here = features.shape[0]
    tiles_here = rows_here // TILE
    members = lax.axis_size("row")
    blocks_per_col = members // lax.axis_size("col")
    cols = rows_here * blocks_per_col
    feat_t = features.T
    noise_2d = noise.reshape(tiles_here, TILE)
    shape = jax.ShapeDtypeStruct
    packed, slot = pl.pallas_call(
        lambda *refs: pack_kernel(tiles_here, *refs),
        out_shape=(shape((members, 2, rows_here + TILE), F32), shape((1,), jnp.int32)),
        in_specs=[sspec(), sspec(), vspec(), vspec()],
        out_specs=(vspec(), sspec()),
        name="pack",
    )(tile_map, panel_tile, feat_t, noise_2d)
    got = lax.all_to_all(packed, "row", 0, 0, tiled=True)
    picked, pivot_noise = pl.pallas_call(
        lambda *refs: pick_kernel(tiles_here, blocks_per_col, *refs),
        out_shape=(shape((members, 2, cols + TILE), F32), shape((1, TILE), F32)),
        in_specs=[sspec(), vspec()],
        out_specs=(vspec(), vspec()),
        name="pick",
    )(slot, got)
    gathered = lax.all_to_all(picked, "row", 0, 0, tiled=True)
    depth = 3 * FEAT + 16
    panel, trailing = pl.pallas_call(
        lambda *refs: step_kernel(tiles_here, *refs),
        grid=(cols // CHUNK,),
        out_shape=(shape((rows_here, TILE), F32), shape((rows_here, cols), F32)),
        in_specs=[sspec(), sspec(), sspec(), vspec(), vspec(), vspec(), vspec()],
        out_specs=(
            pl.BlockSpec((rows_here, TILE), lambda j: (0, 0)),
            pl.BlockSpec((rows_here, CHUNK), lambda j: (0, j)),
        ),
        scratch_shapes=[
            VMEM((FEAT, cols + TILE), F32),
            VMEM((TILE, TILE), F32),
            VMEM((rows_here, depth), BF16),
            VMEM((depth, cols), BF16),
            VMEM((rows_here, 3 * TILE), BF16),
            VMEM((3 * TILE, cols), BF16),
        ],
        compiler_params=pltpu.CompilerParams(vmem_limit_bytes=32 * 1024 * 1024),
        name="step",
    )(tile_map, panel_tile, slot, gathered, pivot_noise, feat_t, noise_2d)
    return panel, trailing


def solution(mesh):
    in_specs = (P("row", None), P("row"), P(), P())
    out_specs = (P("row", None), P("row", "col"))
    return jax.shard_map(shards, mesh=mesh, in_specs=in_specs, out_specs=out_specs, check_vma=False)
```

```python
import jax
import jax.numpy as jnp
from jax import lax
from jax.experimental import pallas as pl
from jax.experimental.pallas import tpu as pltpu
from jax.sharding import PartitionSpec as P

TILE = 128
FEAT = 64
HIGHEST_MODE = lax.Precision.HIGHEST
F32 = jnp.float32
BF16 = jnp.bfloat16
VMEM = pltpu.VMEM
SMEM = pltpu.SMEM
CHUNK = 256
DEPTH = 3 * FEAT + 16
STEP_VMEM = 24 * 1024 * 1024


def vspec():
    return pl.BlockSpec(memory_space=VMEM)


def sspec():
    return pl.BlockSpec(memory_space=SMEM)


def pivot_slot_of(map_ref, panel_ref, tile_count):
    pivot = panel_ref[0]

    def step(s, slot):
        return jnp.where(map_ref[s] == pivot, s, slot)

    return lax.fori_loop(0, tile_count, step, jnp.int32(0), unroll=16)


def pack_kernel(tiles_here, map_ref, panel_ref, feat_ref, noise_ref, out_ref, slot_ref):
    slot = pivot_slot_of(map_ref, panel_ref, map_ref.shape[0])
    slot_ref[0] = slot
    slot_ref[1] = panel_ref[0]
    local = jnp.clip(slot - lax.axis_index("row") * tiles_here, 0, tiles_here - 1)
    rows = feat_ref.shape[1]
    extra = jnp.broadcast_to(noise_ref[pl.ds(local, 1), :], (2, TILE))
    for r in range(out_ref.shape[0]):
        out_ref[r, :, :rows] = feat_ref[2 * r : 2 * r + 2, :]
        out_ref[r, :, rows:] = extra


def pick_kernel(tiles_here, blocks_per_col, slot_ref, got_ref, out_ref, noise_ref):
    slot = slot_ref[0]
    rows = tiles_here * TILE
    first = lax.axis_index("col") * blocks_per_col
    owner = slot // tiles_here
    offset = pl.multiple_of((slot - owner * tiles_here) * TILE, TILE)
    noise_ref[...] = got_ref[owner, 0:1, rows:]
    parts = [got_ref[first + m, :, :rows] for m in range(blocks_per_col)]
    parts.append(got_ref[owner, :, pl.ds(offset, TILE)])
    for r in range(out_ref.shape[0]):
        at = 0
        for part in parts:
            out_ref[r, :, at : at + part.shape[1]] = part
            at += part.shape[1]


def split2(x):
    hi = x.astype(BF16).astype(F32)
    return hi, x - hi


def split3(x):
    a = x.astype(BF16).astype(F32)
    b = (x - a).astype(BF16).astype(F32)
    return a, b, x - a - b


def tail(norm, mine_first):
    n = norm.shape[1]
    at = lax.broadcasted_iota(jnp.int32, (16, n), 0)
    a, b, c = (jnp.broadcast_to(-v, (16, n)) for v in split3(norm))
    base = 0 if mine_first else 3
    out = jnp.where((at >= 3 - base) & (at < 6 - base), 1.0, 0.0)
    for i, v in enumerate((a, b, c)):
        out = jnp.where(at == base + i, v, out)
    return out


def left_side(feat_t):
    norm = jnp.sum(feat_t * feat_t, axis=0, keepdims=True) * (1.0 / FEAT)
    hi, lo = split2(feat_t)
    return jnp.concatenate([hi, hi, lo, tail(norm, True)], axis=0)


def right_side(feat_t):
    norm = jnp.sum(feat_t * feat_t, axis=0, keepdims=True) * (1.0 / FEAT)
    hi, lo = split2(feat_t * (2.0 / FEAT))
    return jnp.concatenate([hi, lo, hi, tail(norm, False)], axis=0).astype(BF16)


def inverse_factor(gram, inv_ref, tasks):
    count = TILE // 8
    full = (8, TILE)
    steps, done = 8 * count, 0
    w = [gram[8 * t : 8 * t + 8, :] for t in range(count)]
    lane = lax.broadcasted_iota(jnp.int32, full, 1)
    sub = lax.broadcasted_iota(jnp.int32, full, 0)
    for b in range(count):
        lo = 8 * b
        inside = (lane >= lo) & (lane < lo + 8)
        c = [jnp.broadcast_to(w[b][:, lo + k : lo + k + 1], full) for k in range(8)]
        r = jnp.where(inside, jnp.where(lane - lo == sub, 1.0, 0.0), w[b])
        out = jnp.zeros(full, F32)
        for s in range(8):
            mine = sub == s
            row = jnp.broadcast_to(r[s : s + 1, :], full)
            piv = jnp.broadcast_to(c[s][s : s + 1, :], full)
            inv = 1.0 / piv
            m = c[s] * inv
            for k in range(s + 1, 8):
                ck = jnp.broadcast_to(c[k][s : s + 1, :], full)
                c[k] = jnp.where(mine, ck * inv, c[k] - m * ck)
            out = jnp.where(mine, row * lax.rsqrt(piv), out)
            r = jnp.where(mine, row * inv, r - m * row)
            upto = len(tasks) * (lo + s + 1) // steps
            for task in tasks[done:upto]:
                task()
            done = upto
        inv_ref[lo : lo + 8, :] = jnp.where(lane < lo + 8, out, 0.0)
        y = [jnp.broadcast_to(r[k : k + 1, :], full) for k in range(8)]
        for t in range(b + 1, count):
            g = [jnp.broadcast_to(w[t][:, lo + k : lo + k + 1], full) * y[k] for k in range(8)]
            total = ((g[0] + g[1]) + (g[2] + g[3])) + ((g[4] + g[5]) + (g[6] + g[7]))
            w[t] = jnp.where(inside, 0.0, w[t]) - total


def dot(a, b, precision=None):
    return jnp.dot(a, b, precision=precision, preferred_element_type=F32)


def left_kernel(feat_ref, left_ref):
    for i in range(feat_ref.shape[1] // TILE):
        here = slice(i * TILE, (i + 1) * TILE)
        left_ref[here, :] = left_side(feat_ref[:, here]).T.astype(BF16)


def step_kernel(
    tiles_here,
    got_ref,
    map_hbm,
    slot_hbm,
    pivot_noise_hbm,
    noise_hbm,
    left_hbm,
    panel_hbm,
    trailing_hbm,
    map_ref,
    slot_ref,
    pivot_noise_ref,
    noise_ref,
    left_ref,
    in_sems,
    all_t,
    inv_ref,
    right_ref,
    row_kern_ref,
    col_kern_ref,
    col_panel_ref,
    row_panel_ref,
    panel_ref,
    out_ref,
    out_sems,
):
    cols = out_ref.shape[1]
    tiles_across = cols // TILE
    loads = [
        pltpu.make_async_copy(src, dst, in_sems.at[n])
        for n, (src, dst) in enumerate(
            (
                (pivot_noise_hbm, pivot_noise_ref),
                (left_hbm, left_ref),
                (map_hbm, map_ref),
                (slot_hbm, slot_ref),
                (noise_hbm, noise_ref),
            )
        )
    ]
    for load in loads:
        load.start()
    first_row_slot = lax.axis_index("row") * tiles_here
    first_col_slot = lax.axis_index("col") * tiles_across
    at_row = lax.broadcasted_iota(jnp.int32, (TILE, TILE), 0)
    at_col = lax.broadcasted_iota(jnp.int32, (TILE, TILE), 1)
    diagonal = at_row == at_col
    for r in range(got_ref.shape[0]):
        all_t[2 * r : 2 * r + 2, :] = got_ref[r]
    pivot_t = all_t[:, cols:]
    pivot_norm = jnp.sum(pivot_t * pivot_t, axis=0, keepdims=True)
    pivot_rows = pivot_t.T
    pivot_norm_col = jnp.sum(pivot_rows * pivot_rows, axis=1, keepdims=True)
    inner = dot(pivot_rows, pivot_t, HIGHEST_MODE)
    gram = jnp.exp((2.0 * inner - pivot_norm_col - pivot_norm) * (1.0 / FEAT))
    pivot_left = left_side(pivot_t).T.astype(BF16)
    pivot_right = right_side(pivot_t)
    for load in loads:
        load.wait()
    slot = slot_ref[0]
    pivot = slot_ref[1]
    pivot_noise = jnp.where(diagonal, pivot_noise_ref[...], 0.0)

    def right_task(j):
        here = slice(j * TILE, (j + 1) * TILE)
        right_ref[:, here] = right_side(all_t[:, here])

    def col_task(j):
        here = slice(j * TILE, (j + 1) * TILE)
        kern = jnp.exp(dot(pivot_left, right_ref[:, here]))
        hi, lo = split2(kern + jnp.where(first_col_slot + j == slot, pivot_noise, 0.0))
        col_kern_ref[:, here] = jnp.concatenate([hi, lo, hi], axis=0).astype(BF16)

    def row_task(i):
        here = slice(i * TILE, (i + 1) * TILE)
        kern = jnp.exp(dot(left_ref[here, :], pivot_right))
        hi, lo = split2(kern + jnp.where(first_row_slot + i == slot, pivot_noise, 0.0))
        row_kern_ref[here, :] = jnp.concatenate([hi, hi, lo], axis=1).astype(BF16)

    def kern_task(i, n):
        here, part = slice(i * TILE, (i + 1) * TILE), slice(n * CHUNK, (n + 1) * CHUNK)
        out_ref[here, part] = jnp.exp(dot(left_ref[here, :], right_ref[:, part]))

    def later(fn, *args):
        return lambda: fn(*args)

    tasks = [later(right_task, j) for j in range(tiles_across)]
    tasks += [later(col_task, j) for j in range(tiles_across)]
    tasks += [later(row_task, i) for i in range(tiles_here)]
    tasks += [later(kern_task, i, n) for n in range(cols // CHUNK) for i in range(tiles_here)]
    inverse_factor(gram + pivot_noise, inv_ref, tasks)

    hi, lo = split2(inv_ref[...])
    inv_left = jnp.concatenate([hi, hi, lo], axis=1).astype(BF16)
    inv_right = jnp.concatenate([hi, lo, hi], axis=1).astype(BF16)
    for i in range(tiles_here):
        here = slice(i * TILE, (i + 1) * TILE)
        factor = lax.dot_general(
            row_kern_ref[here, :],
            inv_right,
            (((1,), (1,)), ((), ())),
            preferred_element_type=F32,
        )
        factor = jnp.where(map_ref[first_row_slot + i] >= pivot, factor, 0.0)
        panel_ref[here, :] = factor
        hi, lo = split2(factor)
        row_panel_ref[here, :] = jnp.concatenate([hi, hi, lo], axis=1).astype(BF16)
    panel_copy = pltpu.make_async_copy(panel_ref, panel_hbm, out_sems.at[0])
    panel_copy.start()
    for n in range(cols // CHUNK):
        part = slice(n * CHUNK, (n + 1) * CHUNK)
        hi, lo = split2(dot(inv_left, col_kern_ref[:, part]))
        col_panel_ref[:, part] = jnp.concatenate([hi, lo, hi], axis=0).astype(BF16)

    ahead = first_row_slot - first_col_slot

    @pl.when((ahead >= 0) & (ahead < tiles_across))
    def _():
        for i in range(tiles_here):
            here = slice(i * TILE, (i + 1) * TILE)
            part = pl.ds(pl.multiple_of((ahead + i) * TILE, TILE), TILE)
            out_ref[here, part] += jnp.where(diagonal, noise_ref[i : i + 1, :], 0.0)

    copies = [panel_copy]
    per_chunk = CHUNK // TILE
    for n in range(cols // CHUNK):
        across = slice(n * CHUNK, (n + 1) * CHUNK)
        for i in range(tiles_here):
            here = slice(i * TILE, (i + 1) * TILE)
            taken = dot(row_panel_ref[here, :], col_panel_ref[:, across])
            row_tile = map_ref[first_row_slot + i]
            for h in range(per_chunk):
                col_tile = map_ref[first_col_slot + n * per_chunk + h]
                live = (row_tile >= col_tile) & (col_tile > pivot)
                part = slice(n * CHUNK + h * TILE, n * CHUNK + (h + 1) * TILE)
                value = out_ref[here, part] - taken[:, h * TILE : (h + 1) * TILE]
                out_ref[here, part] = jnp.where(live, value, 0.0)
        copy = pltpu.make_async_copy(
            out_ref.at[:, across], trailing_hbm.at[:, across], out_sems.at[1 + n]
        )
        copy.start()
        copies.append(copy)
    for copy in copies:
        copy.wait()


def left_call(tiles_here, feat_t):
    rows = tiles_here * TILE
    return pl.pallas_call(
        left_kernel,
        out_shape=jax.ShapeDtypeStruct((rows, DEPTH), BF16),
        in_specs=[vspec()],
        out_specs=vspec(),
        cost_estimate=pl.CostEstimate(flops=10**9, bytes_accessed=5 * 10**6, transcendentals=0),
        name="left",
    )(feat_t)


def step_call(tiles_here, cols, *args):
    rows = tiles_here * TILE
    hspec = pl.BlockSpec(memory_space=pltpu.HBM)
    shape = jax.ShapeDtypeStruct
    return pl.pallas_call(
        lambda *refs: step_kernel(tiles_here, *refs),
        out_shape=(shape((rows, TILE), F32), shape((rows, cols), F32)),
        in_specs=[vspec()] + [hspec] * 5,
        out_specs=(hspec, hspec),
        scratch_shapes=[
            SMEM(args[1].shape, jnp.int32),
            SMEM(args[2].shape, jnp.int32),
            VMEM((1, TILE), F32),
            VMEM((tiles_here, TILE), F32),
            VMEM((rows, DEPTH), BF16),
            pltpu.SemaphoreType.DMA((5,)),
            VMEM((FEAT, cols + TILE), F32),
            VMEM((TILE, TILE), F32),
            VMEM((DEPTH, cols), BF16),
            VMEM((rows, 3 * TILE), BF16),
            VMEM((3 * TILE, cols), BF16),
            VMEM((3 * TILE, cols), BF16),
            VMEM((rows, 3 * TILE), BF16),
            VMEM((rows, TILE), F32),
            VMEM((rows, cols), F32),
            pltpu.SemaphoreType.DMA((1 + cols // CHUNK,)),
        ],
        compiler_params=pltpu.CompilerParams(vmem_limit_bytes=STEP_VMEM),
        name="step",
    )(*args)


def shards(features, noise, tile_map, panel_tile):
    rows_here = features.shape[0]
    tiles_here = rows_here // TILE
    members = lax.axis_size("row")
    blocks_per_col = members // lax.axis_size("col")
    cols = rows_here * blocks_per_col
    feat_t = features.T
    noise_2d = noise.reshape(tiles_here, TILE)
    shape = jax.ShapeDtypeStruct
    packed, slot = pl.pallas_call(
        lambda *refs: pack_kernel(tiles_here, *refs),
        out_shape=(shape((members, 2, rows_here + TILE), F32), shape((2,), jnp.int32)),
        in_specs=[sspec(), sspec(), vspec(), vspec()],
        out_specs=(vspec(), sspec()),
        name="pack",
    )(tile_map, panel_tile, feat_t, noise_2d)
    got = lax.all_to_all(packed, "row", 0, 0, tiled=True)
    picked, pivot_noise = pl.pallas_call(
        lambda *refs: pick_kernel(tiles_here, blocks_per_col, *refs),
        out_shape=(shape((members, 2, cols + TILE), F32), shape((1, TILE), F32)),
        in_specs=[sspec(), vspec()],
        out_specs=(vspec(), vspec()),
        name="pick",
    )(slot, got)
    gathered = lax.all_to_all(picked, "row", 0, 0, tiled=True)
    left = left_call(tiles_here, feat_t)
    held = [
        pltpu.with_memory_space_constraint(x, pltpu.HBM)
        for x in (tile_map, slot, pivot_noise, noise_2d, left)
    ]
    return step_call(tiles_here, cols, gathered, *held)


def solution(mesh):
    in_specs = (P("row", None), P("row"), P(), P())
    out_specs = (P("row", None), P("row", "col"))
    return jax.shard_map(shards, mesh=mesh, in_specs=in_specs, out_specs=out_specs, check_vma=False)
```

```python
import jax
import jax.numpy as jnp
from jax import lax
from jax.experimental import pallas as pl
from jax.experimental.pallas import tpu as pltpu
from jax.sharding import PartitionSpec as P

TILE = 128
FEAT = 64
HIGHEST_MODE = lax.Precision.HIGHEST
F32 = jnp.float32
BF16 = jnp.bfloat16
VMEM = pltpu.VMEM
SMEM = pltpu.SMEM
CHUNK = 256
DEPTH = 3 * FEAT + 16
STEP_VMEM = 24 * 1024 * 1024


def vspec():
    return pl.BlockSpec(memory_space=VMEM)


def sspec():
    return pl.BlockSpec(memory_space=SMEM)


def pivot_slot_of(map_ref, panel_ref, tile_count):
    pivot = panel_ref[0]

    def step(s, slot):
        return jnp.where(map_ref[s] == pivot, s, slot)

    return lax.fori_loop(0, tile_count, step, jnp.int32(0), unroll=True)


def pack_kernel(tiles_here, map_ref, panel_ref, feat_ref, noise_ref, out_ref, slot_ref):
    slot = pivot_slot_of(map_ref, panel_ref, map_ref.shape[0])
    slot_ref[0] = slot
    slot_ref[1] = panel_ref[0]
    local = jnp.clip(slot - lax.axis_index("row") * tiles_here, 0, tiles_here - 1)
    rows = feat_ref.shape[1]
    extra = jnp.broadcast_to(noise_ref[pl.ds(local, 1), :], (2, TILE))
    for r in range(out_ref.shape[0]):
        out_ref[r, :, :rows] = feat_ref[2 * r : 2 * r + 2, :]
        out_ref[r, :, rows:] = extra


def pick_kernel(tiles_here, blocks_per_col, slot_ref, got_ref, out_ref, noise_ref):
    slot = slot_ref[0]
    rows = tiles_here * TILE
    first = lax.axis_index("col") * blocks_per_col
    owner = slot // tiles_here
    offset = pl.multiple_of((slot - owner * tiles_here) * TILE, TILE)
    noise_ref[...] = got_ref[owner, :, rows:]
    parts = [got_ref[first + m, :, :rows] for m in range(blocks_per_col)]
    parts.append(got_ref[owner, :, pl.ds(offset, TILE)])
    for r in range(out_ref.shape[0]):
        at = 0
        for part in parts:
            out_ref[r, :, at : at + part.shape[1]] = part
            at += part.shape[1]


def split2(x):
    hi = x.astype(BF16).astype(F32)
    return hi, x - hi


def split3(x):
    a = x.astype(BF16).astype(F32)
    b = (x - a).astype(BF16).astype(F32)
    return a, b, x - a - b


def tail(norm, mine_first):
    n = norm.shape[1]
    at = lax.broadcasted_iota(jnp.int32, (16, n), 0)
    a, b, c = (jnp.broadcast_to(-v, (16, n)) for v in split3(norm))
    base = 0 if mine_first else 3
    out = jnp.where((at >= 3 - base) & (at < 6 - base), 1.0, 0.0)
    for i, v in enumerate((a, b, c)):
        out = jnp.where(at == base + i, v, out)
    return out


def left_side(feat_t):
    norm = jnp.sum(feat_t * feat_t, axis=0, keepdims=True) * (1.0 / FEAT)
    hi, lo = split2(feat_t)
    return jnp.concatenate([hi, hi, lo, tail(norm, True)], axis=0)


def right_side(feat_t):
    norm = jnp.sum(feat_t * feat_t, axis=0, keepdims=True) * (1.0 / FEAT)
    hi, lo = split2(feat_t * (2.0 / FEAT))
    return jnp.concatenate([hi, lo, hi, tail(norm, False)], axis=0).astype(BF16)


def inverse_factor(gram, inv_ref, tasks):
    count = TILE // 8
    full = (8, TILE)
    steps, done = 4 * count, 0
    w = [gram[8 * t : 8 * t + 8, :] for t in range(count)]
    lane = lax.broadcasted_iota(jnp.int32, full, 1)
    sub = lax.broadcasted_iota(jnp.int32, full, 0)

    def across(v, k):
        return jnp.broadcast_to(v[:, k : k + 1], full)

    def down(v, k):
        return jnp.broadcast_to(v[k : k + 1, :], full)

    for b in range(count):
        lo = 8 * b
        inside = (lane >= lo) & (lane < lo + 8)
        c = [across(w[b], lo + k) for k in range(8)]
        r = jnp.where(inside, jnp.where(lane - lo == sub, 1.0, 0.0), w[b])
        out = jnp.zeros(full, F32)
        for s in range(0, 8, 2):
            first, second = sub == s, sub == s + 1
            row0, row1 = down(r, s), down(r, s + 1)
            p, q, d = down(c[s], s), down(c[s], s + 1), down(c[s + 1], s + 1)
            inv_p = 1.0 / p
            det = p * d - q * q
            inv_det = 1.0 / det
            i00, i01, i11 = d * inv_det, -q * inv_det, p * inv_det
            below = row1 - (q * inv_p) * row0
            out = jnp.where(first, row0 * lax.rsqrt(p), out)
            out = jnp.where(second, below * lax.rsqrt(det * inv_p), out)
            u = jnp.where(second, -i01, c[s] * i00 + c[s + 1] * i01)
            u = jnp.where(first, 1.0 - i00, u)
            v = jnp.where(second, 1.0 - i11, c[s] * i01 + c[s + 1] * i11)
            v = jnp.where(first, -i01, v)
            for k in range(s + 2, 8):
                c[k] = c[k] - (u * down(c[k], s) + v * down(c[k], s + 1))
            r = r - (u * row0 + v * row1)
            upto = len(tasks) * (4 * b + s // 2 + 1) // steps
            for task in tasks[done:upto]:
                task()
            done = upto
        inv_ref[lo : lo + 8, :] = jnp.where(lane < lo + 8, out, 0.0)
        y = [down(r, k) for k in range(8)]
        for t in range(b + 1, count):
            g = [across(w[t], lo + k) * y[k] for k in range(8)]
            total = ((g[0] + g[1]) + (g[2] + g[3])) + ((g[4] + g[5]) + (g[6] + g[7]))
            w[t] = jnp.where(inside, 0.0, w[t]) - total


def dot(a, b, precision=None):
    return jnp.dot(a, b, precision=precision, preferred_element_type=F32)


def step_kernel(
    tiles_here,
    got_ref,
    pivot_noise_ref,
    map_hbm,
    slot_hbm,
    noise_hbm,
    feat_hbm,
    panel_hbm,
    trailing_hbm,
    map_ref,
    slot_ref,
    noise_ref,
    feat_ref,
    left_ref,
    in_sems,
    pivot_t_ref,
    all_t,
    inv_ref,
    right_ref,
    row_kern_ref,
    col_kern_ref,
    col_panel_ref,
    row_panel_ref,
    panel_ref,
    out_ref,
    out_sems,
):
    cols = out_ref.shape[1]
    tiles_across = cols // TILE
    meta_load = pltpu.make_async_copy(slot_hbm, slot_ref, in_sems.at[0])
    meta_load.start()
    loads = [
        pltpu.make_async_copy(src, dst, in_sems.at[1 + n])
        for n, (src, dst) in enumerate(
            ((feat_hbm, feat_ref), (map_hbm, map_ref), (noise_hbm, noise_ref))
        )
    ]
    for load in loads:
        load.start()
    for r in range(got_ref.shape[0]):
        pivot_t_ref[2 * r : 2 * r + 2, :] = got_ref[r, :, cols:]
    first_row_slot = lax.axis_index("row") * tiles_here
    first_col_slot = lax.axis_index("col") * tiles_across
    at_row = lax.broadcasted_iota(jnp.int32, (TILE, TILE), 0)
    at_col = lax.broadcasted_iota(jnp.int32, (TILE, TILE), 1)
    diagonal = at_row == at_col
    pivot_t = pivot_t_ref[...]
    pivot_norm = jnp.sum(pivot_t * pivot_t, axis=0, keepdims=True)
    pivot_rows = pivot_t.T
    pivot_norm_col = jnp.sum(pivot_rows * pivot_rows, axis=1, keepdims=True)
    inner = dot(pivot_rows, pivot_t, HIGHEST_MODE)
    gram = jnp.exp((2.0 * inner - pivot_norm_col - pivot_norm) * (1.0 / FEAT))
    meta_load.wait()
    slot = slot_ref[0]
    pivot = slot_ref[1]
    pivot_noise = jnp.where(diagonal, pivot_noise_ref[0:1, :], 0.0)
    held = {}

    def pivot_task():
        held["left"] = left_side(pivot_t).T.astype(BF16)
        held["right"] = right_side(pivot_t)

    def wait_task():
        for load in loads:
            load.wait()

    def left_task(i):
        here = slice(i * TILE, (i + 1) * TILE)
        left_ref[here, :] = left_side(feat_ref[:, here]).T.astype(BF16)

    def right_task(j):
        here = slice(j * TILE, (j + 1) * TILE)
        for r in range(got_ref.shape[0]):
            all_t[2 * r : 2 * r + 2, here] = got_ref[r, :, here]
        right_ref[:, here] = right_side(all_t[:, here])

    def col_task(j):
        here = slice(j * TILE, (j + 1) * TILE)
        kern = jnp.exp(dot(held["left"], right_ref[:, here]))
        hi, lo = split2(kern + jnp.where(first_col_slot + j == slot, pivot_noise, 0.0))
        col_kern_ref[:, here] = jnp.concatenate([hi, lo, hi], axis=0).astype(BF16)

    def row_task(i):
        here = slice(i * TILE, (i + 1) * TILE)
        kern = jnp.exp(dot(left_ref[here, :], held["right"]))
        hi, lo = split2(kern + jnp.where(first_row_slot + i == slot, pivot_noise, 0.0))
        row_kern_ref[here, :] = jnp.concatenate([hi, hi, lo], axis=1).astype(BF16)

    def kern_task(i, n):
        here, part = slice(i * TILE, (i + 1) * TILE), slice(n * CHUNK, (n + 1) * CHUNK)
        out_ref[here, part] = jnp.exp(dot(left_ref[here, :], right_ref[:, part]))

    def later(fn, *args):
        return lambda: fn(*args)

    tasks = [later(right_task, j) for j in range(tiles_across)] + [pivot_task]
    tasks += [later(col_task, j) for j in range(tiles_across)]
    tasks += [wait_task] + [later(left_task, i) for i in range(tiles_here)]
    tasks += [later(row_task, i) for i in range(tiles_here)]
    tasks += [later(kern_task, i, n) for n in range(cols // CHUNK) for i in range(tiles_here)]
    inverse_factor(gram + pivot_noise, inv_ref, tasks)

    hi, lo = split2(inv_ref[...])
    inv_left = jnp.concatenate([hi, hi, lo], axis=1).astype(BF16)
    inv_right = jnp.concatenate([hi, lo, hi], axis=1).astype(BF16)
    for i in range(tiles_here):
        here = slice(i * TILE, (i + 1) * TILE)
        factor = lax.dot_general(
            row_kern_ref[here, :],
            inv_right,
            (((1,), (1,)), ((), ())),
            preferred_element_type=F32,
        )
        factor = jnp.where(map_ref[first_row_slot + i] >= pivot, factor, 0.0)
        panel_ref[here, :] = factor
        hi, lo = split2(factor)
        row_panel_ref[here, :] = jnp.concatenate([hi, hi, lo], axis=1).astype(BF16)
    panel_copy = pltpu.make_async_copy(panel_ref, panel_hbm, out_sems.at[0])
    panel_copy.start()
    for n in range(cols // CHUNK):
        part = slice(n * CHUNK, (n + 1) * CHUNK)
        hi, lo = split2(dot(inv_left, col_kern_ref[:, part]))
        col_panel_ref[:, part] = jnp.concatenate([hi, lo, hi], axis=0).astype(BF16)

    ahead = first_row_slot - first_col_slot

    @pl.when((ahead >= 0) & (ahead < tiles_across))
    def _():
        for i in range(tiles_here):
            here = slice(i * TILE, (i + 1) * TILE)
            part = pl.ds(pl.multiple_of((ahead + i) * TILE, TILE), TILE)
            out_ref[here, part] += jnp.where(diagonal, noise_ref[i : i + 1, :], 0.0)

    copies = [panel_copy]
    per_chunk = CHUNK // TILE
    for n in range(cols // CHUNK):
        across = slice(n * CHUNK, (n + 1) * CHUNK)
        for i in range(tiles_here):
            here = slice(i * TILE, (i + 1) * TILE)
            taken = dot(row_panel_ref[here, :], col_panel_ref[:, across])
            row_tile = map_ref[first_row_slot + i]
            for h in range(per_chunk):
                col_tile = map_ref[first_col_slot + n * per_chunk + h]
                live = (row_tile >= col_tile) & (col_tile > pivot)
                part = slice(n * CHUNK + h * TILE, n * CHUNK + (h + 1) * TILE)
                value = out_ref[here, part] - taken[:, h * TILE : (h + 1) * TILE]
                out_ref[here, part] = jnp.where(live, value, 0.0)
        copy = pltpu.make_async_copy(
            out_ref.at[:, across], trailing_hbm.at[:, across], out_sems.at[1 + n]
        )
        copy.start()
        copies.append(copy)
    for copy in copies:
        copy.wait()


def step_call(tiles_here, cols, *args):
    rows = tiles_here * TILE
    hspec = pl.BlockSpec(memory_space=pltpu.HBM)
    shape = jax.ShapeDtypeStruct
    return pl.pallas_call(
        lambda *refs: step_kernel(tiles_here, *refs),
        out_shape=(shape((rows, TILE), F32), shape((rows, cols), F32)),
        in_specs=[vspec(), vspec()] + [hspec] * 4,
        out_specs=(hspec, hspec),
        scratch_shapes=[
            SMEM(args[2].shape, jnp.int32),
            SMEM(args[3].shape, jnp.int32),
            VMEM((tiles_here, TILE), F32),
            VMEM((FEAT, rows), F32),
            VMEM((rows, DEPTH), BF16),
            pltpu.SemaphoreType.DMA((4,)),
            VMEM((FEAT, TILE), F32),
            VMEM((FEAT, cols), F32),
            VMEM((TILE, TILE), F32),
            VMEM((DEPTH, cols), BF16),
            VMEM((rows, 3 * TILE), BF16),
            VMEM((3 * TILE, cols), BF16),
            VMEM((3 * TILE, cols), BF16),
            VMEM((rows, 3 * TILE), BF16),
            VMEM((rows, TILE), F32),
            VMEM((rows, cols), F32),
            pltpu.SemaphoreType.DMA((1 + cols // CHUNK,)),
        ],
        compiler_params=pltpu.CompilerParams(vmem_limit_bytes=STEP_VMEM),
        name="step",
    )(*args)


def shards(features, noise, tile_map, panel_tile):
    rows_here = features.shape[0]
    tiles_here = rows_here // TILE
    members = lax.axis_size("row")
    blocks_per_col = members // lax.axis_size("col")
    cols = rows_here * blocks_per_col
    feat_t = features.T
    noise_2d = noise.reshape(tiles_here, TILE)
    shape = jax.ShapeDtypeStruct
    packed, slot = pl.pallas_call(
        lambda *refs: pack_kernel(tiles_here, *refs),
        out_shape=(VMEM((members, 2, rows_here + TILE), F32), shape((2,), jnp.int32)),
        in_specs=[sspec(), sspec(), vspec(), vspec()],
        out_specs=(vspec(), sspec()),
        name="pack",
    )(tile_map, panel_tile, feat_t, noise_2d)
    got = lax.all_to_all(packed, "row", 0, 0, tiled=True)
    got = pltpu.with_memory_space_constraint(got, VMEM)
    picked, pivot_noise = pl.pallas_call(
        lambda *refs: pick_kernel(tiles_here, blocks_per_col, *refs),
        out_shape=(VMEM((members, 2, cols + TILE), F32), VMEM((2, TILE), F32)),
        in_specs=[sspec(), vspec()],
        out_specs=(vspec(), vspec()),
        name="pick",
    )(slot, got)
    gathered = lax.all_to_all(picked, "row", 0, 0, tiled=True)
    held = [
        pltpu.with_memory_space_constraint(x, pltpu.HBM)
        for x in (tile_map, slot, noise_2d, feat_t)
    ]
    return step_call(tiles_here, cols, gathered, pivot_noise, *held)


def solution(mesh):
    in_specs = (P("row", None), P("row"), P(), P())
    out_specs = (P("row", None), P("row", "col"))
    return jax.shard_map(shards, mesh=mesh, in_specs=in_specs, out_specs=out_specs, check_vma=False)
```

```python
import jax
import jax.numpy as jnp
from jax import lax
from jax.experimental import pallas as pl
from jax.experimental.pallas import tpu as pltpu
from jax.sharding import PartitionSpec as P

TILE = 128
FEAT = 64
HIGHEST_MODE = lax.Precision.HIGHEST
F32 = jnp.float32
BF16 = jnp.bfloat16
VMEM = pltpu.VMEM
SMEM = pltpu.SMEM
CHUNK = 256
DEPTH = 3 * FEAT + 16
STEP_VMEM = 24 * 1024 * 1024


def vspec():
    return pl.BlockSpec(memory_space=VMEM)


def sspec():
    return pl.BlockSpec(memory_space=SMEM)


def pivot_slot_of(map_ref, panel_ref, tile_count):
    pivot = panel_ref[0]

    def step(s, slot):
        return jnp.where(map_ref[s] == pivot, s, slot)

    return lax.fori_loop(0, tile_count, step, jnp.int32(0), unroll=True)


def pack_kernel(tiles_here, map_ref, panel_ref, feat_ref, noise_ref, out_ref, slot_ref):
    slot = pivot_slot_of(map_ref, panel_ref, map_ref.shape[0])
    slot_ref[0] = slot
    slot_ref[1] = panel_ref[0]
    local = jnp.clip(slot - lax.axis_index("row") * tiles_here, 0, tiles_here - 1)
    rows = feat_ref.shape[1]
    extra = jnp.broadcast_to(noise_ref[pl.ds(local, 1), :], (2, TILE))
    for r in range(out_ref.shape[0]):
        out_ref[r, :, :rows] = feat_ref[2 * r : 2 * r + 2, :]
        out_ref[r, :, rows:] = extra


def pick_kernel(tiles_here, blocks_per_col, slot_ref, got_ref, out_ref, noise_ref):
    slot = slot_ref[0]
    rows = tiles_here * TILE
    first = lax.axis_index("col") * blocks_per_col
    owner = slot // tiles_here
    offset = pl.multiple_of((slot - owner * tiles_here) * TILE, TILE)
    noise_ref[...] = got_ref[owner, :, rows:]
    parts = [got_ref[first + m, :, :rows] for m in range(blocks_per_col)]
    parts.append(got_ref[owner, :, pl.ds(offset, TILE)])
    for r in range(out_ref.shape[0]):
        at = 0
        for part in parts:
            out_ref[r, :, at : at + part.shape[1]] = part
            at += part.shape[1]


def split2(x):
    hi = x.astype(BF16).astype(F32)
    return hi, x - hi


def split3(x):
    a = x.astype(BF16).astype(F32)
    b = (x - a).astype(BF16).astype(F32)
    return a, b, x - a - b


def tail(norm, mine_first):
    n = norm.shape[1]
    at = lax.broadcasted_iota(jnp.int32, (16, n), 0)
    a, b, c = (jnp.broadcast_to(-v, (16, n)) for v in split3(norm))
    base = 0 if mine_first else 3
    out = jnp.where((at >= 3 - base) & (at < 6 - base), 1.0, 0.0)
    for i, v in enumerate((a, b, c)):
        out = jnp.where(at == base + i, v, out)
    return out


def left_side(feat_t):
    norm = jnp.sum(feat_t * feat_t, axis=0, keepdims=True) * (1.0 / FEAT)
    hi, lo = split2(feat_t)
    return jnp.concatenate([hi, hi, lo, tail(norm, True)], axis=0)


def right_side(feat_t):
    norm = jnp.sum(feat_t * feat_t, axis=0, keepdims=True) * (1.0 / FEAT)
    hi, lo = split2(feat_t * (2.0 / FEAT))
    return jnp.concatenate([hi, lo, hi, tail(norm, False)], axis=0).astype(BF16)


def inverse_factor(gram, inv_ref, tasks):
    count = TILE // 8
    full = (8, TILE)
    steps, done = 4 * count, 0
    w = [gram[8 * t : 8 * t + 8, :] for t in range(count)]
    lane = lax.broadcasted_iota(jnp.int32, full, 1)
    sub = lax.broadcasted_iota(jnp.int32, full, 0)

    def across(v, k):
        return jnp.broadcast_to(v[:, k : k + 1], full)

    def down(v, k):
        return jnp.broadcast_to(v[k : k + 1, :], full)

    for b in range(count):
        lo = 8 * b
        inside = (lane >= lo) & (lane < lo + 8)
        c = [across(w[b], lo + k) for k in range(8)]
        r = jnp.where(inside, jnp.where(lane - lo == sub, 1.0, 0.0), w[b])
        out = jnp.zeros(full, F32)
        for s in range(0, 8, 2):
            first, second = sub == s, sub == s + 1
            row0, row1 = down(r, s), down(r, s + 1)
            p, q, d = down(c[s], s), down(c[s], s + 1), down(c[s + 1], s + 1)
            inv_p = 1.0 / p
            det = p * d - q * q
            inv_det = 1.0 / det
            i00, i01, i11 = d * inv_det, -q * inv_det, p * inv_det
            below = row1 - (q * inv_p) * row0
            out = jnp.where(first, row0 * lax.rsqrt(p), out)
            out = jnp.where(second, below * lax.rsqrt(det * inv_p), out)
            u = jnp.where(second, -i01, c[s] * i00 + c[s + 1] * i01)
            u = jnp.where(first, 1.0 - i00, u)
            v = jnp.where(second, 1.0 - i11, c[s] * i01 + c[s + 1] * i11)
            v = jnp.where(first, -i01, v)
            for k in range(s + 2, 8):
                c[k] = c[k] - (u * down(c[k], s) + v * down(c[k], s + 1))
            r = r - (u * row0 + v * row1)
            upto = max(0, len(tasks) * (4 * b + s // 2 + 1 - steps // 2) // (steps // 2))
            for task in tasks[done:upto]:
                task()
            done = upto
        inv_ref[lo : lo + 8, :] = jnp.where(lane < lo + 8, out, 0.0)
        y = [down(r, k) for k in range(8)]
        for t in range(b + 1, count):
            g = [across(w[t], lo + k) * y[k] for k in range(8)]
            total = ((g[0] + g[1]) + (g[2] + g[3])) + ((g[4] + g[5]) + (g[6] + g[7]))
            w[t] = jnp.where(inside, 0.0, w[t]) - total


def dot(a, b, precision=None):
    return jnp.dot(a, b, precision=precision, preferred_element_type=F32)


def step_kernel(
    tiles_here,
    got_ref,
    pivot_noise_ref,
    map_hbm,
    slot_hbm,
    noise_hbm,
    feat_hbm,
    panel_hbm,
    trailing_hbm,
    map_ref,
    slot_ref,
    noise_ref,
    feat_ref,
    left_ref,
    in_sems,
    pivot_t_ref,
    all_t,
    inv_ref,
    right_ref,
    row_kern_ref,
    col_kern_ref,
    col_panel_ref,
    row_panel_ref,
    panel_ref,
    out_ref,
    out_sems,
):
    cols = out_ref.shape[1]
    tiles_across = cols // TILE
    meta_load = pltpu.make_async_copy(slot_hbm, slot_ref, in_sems.at[0])
    meta_load.start()
    loads = [
        pltpu.make_async_copy(src, dst, in_sems.at[1 + n])
        for n, (src, dst) in enumerate(
            ((feat_hbm, feat_ref), (map_hbm, map_ref), (noise_hbm, noise_ref))
        )
    ]
    for load in loads:
        load.start()
    for r in range(got_ref.shape[0]):
        pivot_t_ref[2 * r : 2 * r + 2, :] = got_ref[r, :, cols:]
    first_row_slot = lax.axis_index("row") * tiles_here
    first_col_slot = lax.axis_index("col") * tiles_across
    at_row = lax.broadcasted_iota(jnp.int32, (TILE, TILE), 0)
    at_col = lax.broadcasted_iota(jnp.int32, (TILE, TILE), 1)
    diagonal = at_row == at_col
    pivot_t = pivot_t_ref[...]
    pivot_norm = jnp.sum(pivot_t * pivot_t, axis=0, keepdims=True)
    pivot_rows = pivot_t.T
    pivot_norm_col = jnp.sum(pivot_rows * pivot_rows, axis=1, keepdims=True)
    inner = dot(pivot_rows, pivot_t, HIGHEST_MODE)
    gram = jnp.exp((2.0 * inner - pivot_norm_col - pivot_norm) * (1.0 / FEAT))
    meta_load.wait()
    slot = slot_ref[0]
    pivot = slot_ref[1]
    pivot_noise = jnp.where(diagonal, pivot_noise_ref[0:1, :], 0.0)
    held = {}

    def pivot_task():
        held["left"] = left_side(pivot_t).T.astype(BF16)
        held["right"] = right_side(pivot_t)

    def wait_task():
        for load in loads:
            load.wait()

    def left_task(i):
        here = slice(i * TILE, (i + 1) * TILE)
        left_ref[here, :] = left_side(feat_ref[:, here]).T.astype(BF16)

    def right_task(j):
        here = slice(j * TILE, (j + 1) * TILE)
        for r in range(got_ref.shape[0]):
            all_t[2 * r : 2 * r + 2, here] = got_ref[r, :, here]
        right_ref[:, here] = right_side(all_t[:, here])

    def col_task(j):
        here = slice(j * TILE, (j + 1) * TILE)
        kern = jnp.exp(dot(held["left"], right_ref[:, here]))
        hi, lo = split2(kern + jnp.where(first_col_slot + j == slot, pivot_noise, 0.0))
        col_kern_ref[:, here] = jnp.concatenate([hi, lo, hi], axis=0).astype(BF16)

    def row_task(i):
        here = slice(i * TILE, (i + 1) * TILE)
        kern = jnp.exp(dot(left_ref[here, :], held["right"]))
        hi, lo = split2(kern + jnp.where(first_row_slot + i == slot, pivot_noise, 0.0))
        row_kern_ref[here, :] = jnp.concatenate([hi, hi, lo], axis=1).astype(BF16)

    def kern_task(i, n):
        here, part = slice(i * TILE, (i + 1) * TILE), slice(n * CHUNK, (n + 1) * CHUNK)
        out_ref[here, part] = jnp.exp(dot(left_ref[here, :], right_ref[:, part]))

    def later(fn, *args):
        return lambda: fn(*args)

    tasks = [later(right_task, j) for j in range(tiles_across)] + [pivot_task]
    tasks += [later(col_task, j) for j in range(tiles_across)]
    tasks += [wait_task] + [later(left_task, i) for i in range(tiles_here)]
    tasks += [later(row_task, i) for i in range(tiles_here)]
    tasks += [later(kern_task, i, n) for n in range(cols // CHUNK) for i in range(tiles_here)]
    inverse_factor(gram + pivot_noise, inv_ref, tasks)

    hi, lo = split2(inv_ref[...])
    inv_left = jnp.concatenate([hi, hi, lo], axis=1).astype(BF16)
    inv_right = jnp.concatenate([hi, lo, hi], axis=1).astype(BF16)
    for i in range(tiles_here):
        here = slice(i * TILE, (i + 1) * TILE)
        factor = lax.dot_general(
            row_kern_ref[here, :],
            inv_right,
            (((1,), (1,)), ((), ())),
            preferred_element_type=F32,
        )
        factor = jnp.where(map_ref[first_row_slot + i] >= pivot, factor, 0.0)
        panel_ref[here, :] = factor
        hi, lo = split2(factor)
        row_panel_ref[here, :] = jnp.concatenate([hi, hi, lo], axis=1).astype(BF16)
    panel_copy = pltpu.make_async_copy(panel_ref, panel_hbm, out_sems.at[0])
    panel_copy.start()
    for n in range(cols // CHUNK):
        part = slice(n * CHUNK, (n + 1) * CHUNK)
        hi, lo = split2(dot(inv_left, col_kern_ref[:, part]))
        col_panel_ref[:, part] = jnp.concatenate([hi, lo, hi], axis=0).astype(BF16)

    ahead = first_row_slot - first_col_slot

    @pl.when((ahead >= 0) & (ahead < tiles_across))
    def _():
        for i in range(tiles_here):
            here = slice(i * TILE, (i + 1) * TILE)
            part = pl.ds(pl.multiple_of((ahead + i) * TILE, TILE), TILE)
            out_ref[here, part] += jnp.where(diagonal, noise_ref[i : i + 1, :], 0.0)

    copies = [panel_copy]
    per_chunk = CHUNK // TILE
    for n in range(cols // CHUNK):
        across = slice(n * CHUNK, (n + 1) * CHUNK)
        for i in range(tiles_here):
            here = slice(i * TILE, (i + 1) * TILE)
            taken = dot(row_panel_ref[here, :], col_panel_ref[:, across])
            row_tile = map_ref[first_row_slot + i]
            for h in range(per_chunk):
                col_tile = map_ref[first_col_slot + n * per_chunk + h]
                live = (row_tile >= col_tile) & (col_tile > pivot)
                part = slice(n * CHUNK + h * TILE, n * CHUNK + (h + 1) * TILE)
                value = out_ref[here, part] - taken[:, h * TILE : (h + 1) * TILE]
                out_ref[here, part] = jnp.where(live, value, 0.0)
        copy = pltpu.make_async_copy(
            out_ref.at[:, across], trailing_hbm.at[:, across], out_sems.at[1 + n]
        )
        copy.start()
        copies.append(copy)
    for copy in copies:
        copy.wait()


def step_call(tiles_here, cols, *args):
    rows = tiles_here * TILE
    hspec = pl.BlockSpec(memory_space=pltpu.HBM)
    shape = jax.ShapeDtypeStruct
    return pl.pallas_call(
        lambda *refs: step_kernel(tiles_here, *refs),
        out_shape=(shape((rows, TILE), F32), shape((rows, cols), F32)),
        in_specs=[vspec(), vspec()] + [hspec] * 4,
        out_specs=(hspec, hspec),
        scratch_shapes=[
            SMEM(args[2].shape, jnp.int32),
            SMEM(args[3].shape, jnp.int32),
            VMEM((tiles_here, TILE), F32),
            VMEM((FEAT, rows), F32),
            VMEM((rows, DEPTH), BF16),
            pltpu.SemaphoreType.DMA((4,)),
            VMEM((FEAT, TILE), F32),
            VMEM((FEAT, cols), F32),
            VMEM((TILE, TILE), F32),
            VMEM((DEPTH, cols), BF16),
            VMEM((rows, 3 * TILE), BF16),
            VMEM((3 * TILE, cols), BF16),
            VMEM((3 * TILE, cols), BF16),
            VMEM((rows, 3 * TILE), BF16),
            VMEM((rows, TILE), F32),
            VMEM((rows, cols), F32),
            pltpu.SemaphoreType.DMA((1 + cols // CHUNK,)),
        ],
        compiler_params=pltpu.CompilerParams(vmem_limit_bytes=STEP_VMEM),
        name="step",
    )(*args)


def shards(features, noise, tile_map, panel_tile):
    rows_here = features.shape[0]
    tiles_here = rows_here // TILE
    members = lax.axis_size("row")
    blocks_per_col = members // lax.axis_size("col")
    cols = rows_here * blocks_per_col
    feat_t = features.T
    noise_2d = noise.reshape(tiles_here, TILE)
    shape = jax.ShapeDtypeStruct
    packed, slot = pl.pallas_call(
        lambda *refs: pack_kernel(tiles_here, *refs),
        out_shape=(VMEM((members, 2, rows_here + TILE), F32), shape((2,), jnp.int32)),
        in_specs=[sspec(), sspec(), vspec(), vspec()],
        out_specs=(vspec(), sspec()),
        name="pack",
    )(tile_map, panel_tile, feat_t, noise_2d)
    got = lax.all_to_all(packed, "row", 0, 0, tiled=True)
    got = pltpu.with_memory_space_constraint(got, VMEM)
    picked, pivot_noise = pl.pallas_call(
        lambda *refs: pick_kernel(tiles_here, blocks_per_col, *refs),
        out_shape=(VMEM((members, 2, cols + TILE), F32), VMEM((2, TILE), F32)),
        in_specs=[sspec(), vspec()],
        out_specs=(vspec(), vspec()),
        name="pick",
    )(slot, got)
    gathered = lax.all_to_all(picked, "row", 0, 0, tiled=True)
    held = [
        pltpu.with_memory_space_constraint(x, pltpu.HBM)
        for x in (tile_map, slot, noise_2d, feat_t)
    ]
    return step_call(tiles_here, cols, gathered, pivot_noise, *held)


def solution(mesh):
    in_specs = (P("row", None), P("row"), P(), P())
    out_specs = (P("row", None), P("row", "col"))
    return jax.shard_map(shards, mesh=mesh, in_specs=in_specs, out_specs=out_specs, check_vma=False)
```

```python
import jax
import jax.numpy as jnp
from jax import lax
from jax.experimental import pallas as pl
from jax.experimental.pallas import tpu as pltpu
from jax.sharding import PartitionSpec as P

TILE = 128
FEAT = 64
HIGHEST_MODE = lax.Precision.HIGHEST
F32 = jnp.float32
BF16 = jnp.bfloat16
VMEM = pltpu.VMEM
SMEM = pltpu.SMEM
CHUNK = 256
TASK_CHUNKS = 3
IDLE_STEPS = 28
DEPTH = 3 * FEAT + 16
STEP_VMEM = 24 * 1024 * 1024


def vspec():
    return pl.BlockSpec(memory_space=VMEM)


def sspec():
    return pl.BlockSpec(memory_space=SMEM)


def pivot_slot_of(map_ref, panel_ref, tile_count):
    pivot = panel_ref[0]

    def step(s, slot):
        return jnp.where(map_ref[s] == pivot, s, slot)

    return lax.fori_loop(0, tile_count, step, jnp.int32(0), unroll=True)


def pack_kernel(tiles_here, map_ref, panel_ref, feat_ref, noise_ref, out_ref, slot_ref):
    slot = pivot_slot_of(map_ref, panel_ref, map_ref.shape[0])
    slot_ref[0] = slot
    slot_ref[1] = panel_ref[0]
    local = jnp.clip(slot - lax.axis_index("row") * tiles_here, 0, tiles_here - 1)
    rows = feat_ref.shape[1]
    extra = jnp.broadcast_to(noise_ref[pl.ds(local, 1), :], (2, TILE))
    for r in range(out_ref.shape[0]):
        out_ref[r, :, :rows] = feat_ref[2 * r : 2 * r + 2, :]
        out_ref[r, :, rows:] = extra


def pick_kernel(tiles_here, blocks_per_col, slot_ref, got_ref, out_ref, noise_ref):
    slot = slot_ref[0]
    rows = tiles_here * TILE
    first = lax.axis_index("col") * blocks_per_col
    owner = slot // tiles_here
    offset = pl.multiple_of((slot - owner * tiles_here) * TILE, TILE)
    noise_ref[...] = got_ref[owner, :, rows:]
    parts = [got_ref[first + m, :, :rows] for m in range(blocks_per_col)]
    parts.append(got_ref[owner, :, pl.ds(offset, TILE)])
    for r in range(out_ref.shape[0]):
        at = 0
        for part in parts:
            out_ref[r, :, at : at + part.shape[1]] = part
            at += part.shape[1]


def split2(x):
    hi = x.astype(BF16).astype(F32)
    return hi, x - hi


def split3(x):
    a = x.astype(BF16).astype(F32)
    b = (x - a).astype(BF16).astype(F32)
    return a, b, x - a - b


def tail(norm, mine_first):
    n = norm.shape[1]
    at = lax.broadcasted_iota(jnp.int32, (16, n), 0)
    a, b, c = (jnp.broadcast_to(-v, (16, n)) for v in split3(norm))
    base = 0 if mine_first else 3
    out = jnp.where((at >= 3 - base) & (at < 6 - base), 1.0, 0.0)
    for i, v in enumerate((a, b, c)):
        out = jnp.where(at == base + i, v, out)
    return out


def left_side(feat_t):
    norm = jnp.sum(feat_t * feat_t, axis=0, keepdims=True) * (1.0 / FEAT)
    hi, lo = split2(feat_t)
    return jnp.concatenate([hi, hi, lo, tail(norm, True)], axis=0)


def right_side(feat_t):
    norm = jnp.sum(feat_t * feat_t, axis=0, keepdims=True) * (1.0 / FEAT)
    hi, lo = split2(feat_t * (2.0 / FEAT))
    return jnp.concatenate([hi, lo, hi, tail(norm, False)], axis=0).astype(BF16)


def inverse_factor(gram, inv_ref, tasks):
    count = TILE // 8
    full = (8, TILE)
    steps, done = 4 * count, 0
    w = [gram[8 * t : 8 * t + 8, :] for t in range(count)]
    lane = lax.broadcasted_iota(jnp.int32, full, 1)
    sub = lax.broadcasted_iota(jnp.int32, full, 0)

    def across(v, k):
        return jnp.broadcast_to(v[:, k : k + 1], full)

    def down(v, k):
        return jnp.broadcast_to(v[k : k + 1, :], full)

    for b in range(count):
        lo = 8 * b
        inside = (lane >= lo) & (lane < lo + 8)
        c = [across(w[b], lo + k) for k in range(8)]
        r = jnp.where(inside, jnp.where(lane - lo == sub, 1.0, 0.0), w[b])
        out = jnp.zeros(full, F32)
        for s in range(0, 8, 2):
            first, second = sub == s, sub == s + 1
            row0, row1 = down(r, s), down(r, s + 1)
            p, q, d = down(c[s], s), down(c[s], s + 1), down(c[s + 1], s + 1)
            inv_p = 1.0 / p
            det = p * d - q * q
            inv_det = 1.0 / det
            i00, i01, i11 = d * inv_det, -q * inv_det, p * inv_det
            below = row1 - (q * inv_p) * row0
            out = jnp.where(first, row0 * lax.rsqrt(p), out)
            out = jnp.where(second, below * lax.rsqrt(det * inv_p), out)
            u = jnp.where(second, -i01, c[s] * i00 + c[s + 1] * i01)
            u = jnp.where(first, 1.0 - i00, u)
            v = jnp.where(second, 1.0 - i11, c[s] * i01 + c[s + 1] * i11)
            v = jnp.where(first, -i01, v)
            for k in range(s + 2, 8):
                c[k] = c[k] - (u * down(c[k], s) + v * down(c[k], s + 1))
            r = r - (u * row0 + v * row1)
            upto = max(0, len(tasks) * (4 * b + s // 2 + 1 - IDLE_STEPS) // (steps - IDLE_STEPS))
            for task in tasks[done:upto]:
                task()
            done = upto
        inv_ref[lo : lo + 8, :] = jnp.where(lane < lo + 8, out, 0.0)
        y = [down(r, k) for k in range(8)]
        for t in range(b + 1, count):
            g = [across(w[t], lo + k) * y[k] for k in range(8)]
            total = ((g[0] + g[1]) + (g[2] + g[3])) + ((g[4] + g[5]) + (g[6] + g[7]))
            w[t] = jnp.where(inside, 0.0, w[t]) - total


def dot(a, b, precision=None):
    return jnp.dot(a, b, precision=precision, preferred_element_type=F32)


def step_kernel(
    tiles_here,
    got_ref,
    pivot_noise_ref,
    map_hbm,
    slot_hbm,
    noise_hbm,
    feat_hbm,
    panel_hbm,
    trailing_hbm,
    map_ref,
    slot_ref,
    noise_ref,
    feat_ref,
    left_ref,
    in_sems,
    pivot_t_ref,
    all_t,
    inv_ref,
    right_ref,
    row_kern_ref,
    col_kern_ref,
    col_panel_ref,
    row_panel_ref,
    panel_ref,
    out_ref,
    out_sems,
):
    cols = out_ref.shape[1]
    tiles_across = cols // TILE
    meta_load = pltpu.make_async_copy(slot_hbm, slot_ref, in_sems.at[0])
    meta_load.start()
    loads = [
        pltpu.make_async_copy(src, dst, in_sems.at[1 + n])
        for n, (src, dst) in enumerate(
            ((feat_hbm, feat_ref), (map_hbm, map_ref), (noise_hbm, noise_ref))
        )
    ]
    for load in loads:
        load.start()
    for r in range(got_ref.shape[0]):
        pivot_t_ref[2 * r : 2 * r + 2, :] = got_ref[r, :, cols:]
    first_row_slot = lax.axis_index("row") * tiles_here
    first_col_slot = lax.axis_index("col") * tiles_across
    at_row = lax.broadcasted_iota(jnp.int32, (TILE, TILE), 0)
    at_col = lax.broadcasted_iota(jnp.int32, (TILE, TILE), 1)
    diagonal = at_row == at_col
    pivot_t = pivot_t_ref[...]
    pivot_norm = jnp.sum(pivot_t * pivot_t, axis=0, keepdims=True)
    pivot_rows = pivot_t.T
    pivot_norm_col = jnp.sum(pivot_rows * pivot_rows, axis=1, keepdims=True)
    inner = dot(pivot_rows, pivot_t, HIGHEST_MODE)
    gram = jnp.exp((2.0 * inner - pivot_norm_col - pivot_norm) * (1.0 / FEAT))
    meta_load.wait()
    slot = slot_ref[0]
    pivot = slot_ref[1]
    pivot_noise = jnp.where(diagonal, pivot_noise_ref[0:1, :], 0.0)
    held = {}

    def pivot_task():
        held["left"] = left_side(pivot_t).T.astype(BF16)
        held["right"] = right_side(pivot_t)

    def wait_task():
        for load in loads:
            load.wait()

    def left_task(i):
        here = slice(i * TILE, (i + 1) * TILE)
        left_ref[here, :] = left_side(feat_ref[:, here]).T.astype(BF16)

    def right_task(j):
        here = slice(j * TILE, (j + 1) * TILE)
        for r in range(got_ref.shape[0]):
            all_t[2 * r : 2 * r + 2, here] = got_ref[r, :, here]
        right_ref[:, here] = right_side(all_t[:, here])

    def col_task(j):
        here = slice(j * TILE, (j + 1) * TILE)
        kern = jnp.exp(dot(held["left"], right_ref[:, here]))
        hi, lo = split2(kern + jnp.where(first_col_slot + j == slot, pivot_noise, 0.0))
        col_kern_ref[:, here] = jnp.concatenate([hi, lo, hi], axis=0).astype(BF16)

    def row_task(i):
        here = slice(i * TILE, (i + 1) * TILE)
        kern = jnp.exp(dot(left_ref[here, :], held["right"]))
        hi, lo = split2(kern + jnp.where(first_row_slot + i == slot, pivot_noise, 0.0))
        row_kern_ref[here, :] = jnp.concatenate([hi, hi, lo], axis=1).astype(BF16)

    def kern_task(i, n):
        here, part = slice(i * TILE, (i + 1) * TILE), slice(n * CHUNK, (n + 1) * CHUNK)
        out_ref[here, part] = jnp.exp(dot(left_ref[here, :], right_ref[:, part]))

    def later(fn, *args):
        return lambda: fn(*args)

    tasks = [later(right_task, j) for j in range(tiles_across)] + [pivot_task]
    tasks += [later(col_task, j) for j in range(tiles_across)]
    tasks += [wait_task] + [later(left_task, i) for i in range(tiles_here)]
    tasks += [later(row_task, i) for i in range(tiles_here)]
    tasks += [later(kern_task, i, n) for n in range(TASK_CHUNKS) for i in range(tiles_here)]
    inverse_factor(gram + pivot_noise, inv_ref, tasks)

    hi, lo = split2(inv_ref[...])
    inv_left = jnp.concatenate([hi, hi, lo], axis=1).astype(BF16)
    inv_right = jnp.concatenate([hi, lo, hi], axis=1).astype(BF16)
    for i in range(tiles_here):
        here = slice(i * TILE, (i + 1) * TILE)
        factor = lax.dot_general(
            row_kern_ref[here, :],
            inv_right,
            (((1,), (1,)), ((), ())),
            preferred_element_type=F32,
        )
        factor = jnp.where(map_ref[first_row_slot + i] >= pivot, factor, 0.0)
        panel_ref[here, :] = factor
        hi, lo = split2(factor)
        row_panel_ref[here, :] = jnp.concatenate([hi, hi, lo], axis=1).astype(BF16)
    panel_copy = pltpu.make_async_copy(panel_ref, panel_hbm, out_sems.at[0])
    panel_copy.start()
    for n in range(cols // CHUNK):
        part = slice(n * CHUNK, (n + 1) * CHUNK)
        hi, lo = split2(dot(inv_left, col_kern_ref[:, part]))
        col_panel_ref[:, part] = jnp.concatenate([hi, lo, hi], axis=0).astype(BF16)

    ahead = first_row_slot - first_col_slot

    @pl.when((ahead >= 0) & (ahead < tiles_across))
    def _():
        for i in range(tiles_here):
            here = slice(i * TILE, (i + 1) * TILE)
            part = pl.ds(pl.multiple_of((ahead + i) * TILE, TILE), TILE)


            @pl.when(ahead + i < TASK_CHUNKS * (CHUNK // TILE))
            def _():
                out_ref[here, part] += jnp.where(diagonal, noise_ref[i : i + 1, :], 0.0)

    copies = [panel_copy]
    per_chunk = CHUNK // TILE
    for n in range(cols // CHUNK):
        across = slice(n * CHUNK, (n + 1) * CHUNK)
        for i in range(tiles_here):
            here = slice(i * TILE, (i + 1) * TILE)
            taken = dot(row_panel_ref[here, :], col_panel_ref[:, across])
            kern = jnp.exp(dot(left_ref[here, :], right_ref[:, across])) if n >= TASK_CHUNKS else None
            row_tile = map_ref[first_row_slot + i]
            for h in range(per_chunk):
                col_tile = map_ref[first_col_slot + n * per_chunk + h]
                live = (row_tile >= col_tile) & (col_tile > pivot)
                part = slice(n * CHUNK + h * TILE, n * CHUNK + (h + 1) * TILE)
                value = (kern[:, h * TILE : (h + 1) * TILE] if n >= TASK_CHUNKS else out_ref[here, part]) - taken[:, h * TILE : (h + 1) * TILE]
                out_ref[here, part] = jnp.where(live, value, 0.0)
        if n >= TASK_CHUNKS:

            @pl.when((ahead >= 0) & (ahead < tiles_across))
            def _():
                for h in range(per_chunk):
                    i = n * per_chunk + h - ahead

                    @pl.when((i >= 0) & (i < tiles_here))
                    def _():
                        here = pl.ds(pl.multiple_of(i * TILE, TILE), TILE)
                        part = slice(n * CHUNK + h * TILE, n * CHUNK + (h + 1) * TILE)
                        live = map_ref[first_row_slot + i] > pivot
                        own = jnp.where(diagonal, noise_ref[pl.ds(i, 1), :], 0.0)
                        out_ref[here, part] += jnp.where(live, own, 0.0)

        copy = pltpu.make_async_copy(
            out_ref.at[:, across], trailing_hbm.at[:, across], out_sems.at[1 + n]
        )
        copy.start()
        copies.append(copy)
    for copy in copies:
        copy.wait()


def step_call(tiles_here, cols, *args):
    rows = tiles_here * TILE
    hspec = pl.BlockSpec(memory_space=pltpu.HBM)
    shape = jax.ShapeDtypeStruct
    return pl.pallas_call(
        lambda *refs: step_kernel(tiles_here, *refs),
        out_shape=(shape((rows, TILE), F32), shape((rows, cols), F32)),
        in_specs=[vspec(), vspec()] + [hspec] * 4,
        out_specs=(hspec, hspec),
        scratch_shapes=[
            SMEM(args[2].shape, jnp.int32),
            SMEM(args[3].shape, jnp.int32),
            VMEM((tiles_here, TILE), F32),
            VMEM((FEAT, rows), F32),
            VMEM((rows, DEPTH), BF16),
            pltpu.SemaphoreType.DMA((4,)),
            VMEM((FEAT, TILE), F32),
            VMEM((FEAT, cols), F32),
            VMEM((TILE, TILE), F32),
            VMEM((DEPTH, cols), BF16),
            VMEM((rows, 3 * TILE), BF16),
            VMEM((3 * TILE, cols), BF16),
            VMEM((3 * TILE, cols), BF16),
            VMEM((rows, 3 * TILE), BF16),
            VMEM((rows, TILE), F32),
            VMEM((rows, cols), F32),
            pltpu.SemaphoreType.DMA((1 + cols // CHUNK,)),
        ],
        compiler_params=pltpu.CompilerParams(vmem_limit_bytes=STEP_VMEM),
        name="step",
    )(*args)


def shards(features, noise, tile_map, panel_tile):
    rows_here = features.shape[0]
    tiles_here = rows_here // TILE
    members = lax.axis_size("row")
    blocks_per_col = members // lax.axis_size("col")
    cols = rows_here * blocks_per_col
    feat_t = features.T
    noise_2d = noise.reshape(tiles_here, TILE)
    shape = jax.ShapeDtypeStruct
    packed, slot = pl.pallas_call(
        lambda *refs: pack_kernel(tiles_here, *refs),
        out_shape=(VMEM((members, 2, rows_here + TILE), F32), shape((2,), jnp.int32)),
        in_specs=[sspec(), sspec(), vspec(), vspec()],
        out_specs=(vspec(), sspec()),
        name="pack",
    )(tile_map, panel_tile, feat_t, noise_2d)
    got = lax.all_to_all(packed, "row", 0, 0, tiled=True)
    got = pltpu.with_memory_space_constraint(got, VMEM)
    picked, pivot_noise = pl.pallas_call(
        lambda *refs: pick_kernel(tiles_here, blocks_per_col, *refs),
        out_shape=(VMEM((members, 2, cols + TILE), F32), VMEM((2, TILE), F32)),
        in_specs=[sspec(), vspec()],
        out_specs=(vspec(), vspec()),
        name="pick",
    )(slot, got)
    gathered = lax.all_to_all(picked, "row", 0, 0, tiled=True)
    held = [
        pltpu.with_memory_space_constraint(x, pltpu.HBM)
        for x in (tile_map, slot, noise_2d, feat_t)
    ]
    return step_call(tiles_here, cols, gathered, pivot_noise, *held)


def solution(mesh):
    in_specs = (P("row", None), P("row"), P(), P())
    out_specs = (P("row", None), P("row", "col"))
    return jax.shard_map(shards, mesh=mesh, in_specs=in_specs, out_specs=out_specs, check_vma=False)
```
